32 devices in a mesh: node: 4 (over y, x), span: 8 (over z, core).
Axes of the slice: x: 2, y: 2, z: 4, core: 2. Of those that a mesh axis runs over, the one named last changes fastest.
Arguments:
- iterate: float32 [4, 2, 576, 4608], P('node', None, None, 'span'), may hold values from -6 to 6
- start_field: float32 [2, 576, 4608], P(None, None, 'span'), may hold values from -6 to 6
- spanwise_velocity: float32 [4, 576, 4608], P('node', 'span'), may hold values from -6 to 6
- eigen_basis: float32 [576, 576], replicated, may hold values from -3 to 3
- inverse_basis: float32 [576, 576], replicated, may hold values from -3 to 3, as said below
- decay_rates: float32 [576], replicated, may hold values from 0.05 to 5
Outputs:
- updated: float32 [4, 2, 576, 4608], P('node', None, None, 'span')
The draws below stay inside these ranges and needn't reach their ends.
Inputs may be any that keep to these rules, and one draw needn't show every extreme that they name: inverse_basis is the inverse of eigen_basis up to float32 rounding.
All inputs are finite; a program needn't handle non-finite values.
Results may differ from the reference program's by a relative error of at most 0.00054.
Values may be sent and summed in bfloat16 or wider, within the bound.
No kernel may reach another device: no remote copies, remote signals or barrier semaphores. Data moves between devices by JAX's collectives and lax.ppermute only.
A program may use at most 64 MiB of HBM per device.

```python
import math
import jax
import jax.numpy as jnp
from jax import lax

NY = 576
NZ = 4608
NODES = 4


def basis_pair(key):
    branch_key = jax.random.fold_in(key, 41)
    identity = jnp.eye(NY, dtype=jnp.float32)
    spread = 0.3 * jax.random.truncated_normal(branch_key, -3.0, 3.0, (NY, NY), jnp.float32)
    matrix = identity + spread / jnp.sqrt(jnp.float32(NY))
    inverse = jnp.linalg.solve(matrix, identity)
    return (matrix, inverse)


def draw_eigen_basis(key, part):
    return basis_pair(key)[0]


def draw_inverse_basis(key, part):
    return basis_pair(key)[1]


def block_scale(own_key, extent, shards, smallest, high):
    loudness = 1.0
    for position, shards_of in shards:
        steps = jax.random.uniform(jax.random.fold_in(jax.random.fold_in(own_key, 6), position), (shards_of,), jnp.float32, smallest / len(shards), high / len(shards))
        loudness = loudness * jnp.repeat(jnp.exp(steps), extent[position] // shards_of).reshape((-1,) + (1,) * (len(extent) - 1 - position))
    return loudness


def bell_draw(key, extent, width, limit, pieces=(), kind=jnp.bfloat16):
    entries = jax.random.normal(key, extent, jnp.float32) * width
    if len(pieces) > 0:
        entries = block_scale(key, extent, pieces, -0.22, 0.18) * entries
    return jnp.clip(entries, min=-limit, max=limit).astype(kind)


def setup_inputs(seed: int = 0) -> dict:
    splits = jax.random.split(jax.random.key(seed), 7)
    iterate = bell_draw(splits[0], (NODES, 2, NY, NZ), 1.0, 6.0, ((0, 4), (3, 8)), jnp.float32)
    start_field = bell_draw(splits[1], (2, NY, NZ), 1.0, 6.0, ((2, 8),), jnp.float32)
    spanwise_velocity = bell_draw(splits[2], (NODES, NY, NZ), 1.0, 6.0, ((0, 4), (1, 8)), jnp.float32)
    eigen_basis = draw_eigen_basis(jax.random.fold_in(splits[6], 71), 0)
    inverse_basis = draw_inverse_basis(jax.random.fold_in(splits[6], 71), 0)
    decay_rates = jnp.clip(jnp.exp(jax.random.uniform(splits[5], (NY,), jnp.float32, math.log(0.05), math.log(5.0))), 0.05, 5.0)
    return {"iterate": iterate, "start_field": start_field, "spanwise_velocity": spanwise_velocity, "eigen_basis": eigen_basis, "inverse_basis": inverse_basis, "decay_rates": decay_rates}


def collocation(node_total):
    points = [0.5 - 0.5 * math.cos((2.0 * m + 1.0) * math.pi / (2.0 * node_total)) for m in range(node_total)]
    weights = [[0.0] * node_total for _ in range(node_total)]
    for column in range(node_total):
        coeffs = [1.0]
        scale = 1.0
        for other in range(node_total):
            if other != column:
                grown = [0.0] * (len(coeffs) + 1)
                for power in range(len(coeffs)):
                    grown[power + 1] += coeffs[power]
                    grown[power] -= points[other] * coeffs[power]
                coeffs = grown
                scale = scale * (points[column] - points[other])
        for row in range(node_total):
            total = 0.0
            for power in range(len(coeffs)):
                total += coeffs[power] * points[row] ** (power + 1) / (power + 1)
            weights[row][column] = total / scale
    return (weights, [value / node_total for value in points])

def reference(iterate, start_field, spanwise_velocity, eigen_basis, inverse_basis, decay_rates):
    highest = lax.Precision.HIGHEST
    quadrature_table, shift_table = collocation(NODES)
    quadrature = jnp.asarray(quadrature_table, jnp.float32)
    shifts = jnp.asarray(shift_table, jnp.float32)
    wavenumber = jnp.arange(NZ, dtype=jnp.int32)
    signed = jnp.where(wavenumber < NZ // 2, wavenumber, wavenumber - NZ).astype(jnp.float32) / (NZ // 2)
    damping = decay_rates[:, None] + signed[None, :] ** 2
    gradient_real = lax.optimization_barrier((-signed * iterate[:, 1]).astype(jnp.bfloat16)).astype(jnp.float32)
    gradient_imaginary = lax.optimization_barrier((signed * iterate[:, 0]).astype(jnp.bfloat16)).astype(jnp.float32)
    physical = jnp.fft.ifft(lax.complex(gradient_real, gradient_imaginary), axis=-1, norm='ortho')
    spectral = jnp.fft.fft(-spanwise_velocity * physical, axis=-1, norm='ortho')
    advect = jnp.stack([jnp.real(spectral), jnp.imag(spectral)], axis=1)
    advect = lax.optimization_barrier(advect.astype(jnp.bfloat16)).astype(jnp.float32)
    coefficients = jnp.einsum('yx,mcxq->mcyq', inverse_basis, iterate, precision=highest)
    start_coeff = jnp.einsum('yx,cxq->cyq', inverse_basis, start_field, precision=highest)
    section_term = -damping * coefficients + jnp.einsum('yx,mcxq->mcyq', inverse_basis, advect, precision=highest)
    summed = jnp.einsum('mj,jcyq->mcyq', quadrature, section_term, precision=highest)
    node_shift = shifts[:, None, None, None] * damping
    new_coeff = (start_coeff[None] + summed + node_shift * coefficients) / (1.0 + node_shift)
    return jnp.einsum('yx,mcxq->mcyq', eigen_basis, new_coeff, precision=highest)
```

```python
import functools
import math

import jax
import jax.numpy as jnp
import numpy as np
from jax import lax
from jax.experimental import pallas as pl
from jax.experimental.pallas import tpu as pltpu
from jax.sharding import PartitionSpec as P


def collocation(node_total):
    points = [
        0.5 - 0.5 * math.cos((2.0 * m + 1.0) * math.pi / (2.0 * node_total))
        for m in range(node_total)
    ]
    weights = [[0.0] * node_total for _ in range(node_total)]
    for column in range(node_total):
        coeffs = [1.0]
        scale = 1.0
        for other in range(node_total):
            if other != column:
                grown = [0.0] * (len(coeffs) + 1)
                for power in range(len(coeffs)):
                    grown[power + 1] += coeffs[power]
                    grown[power] -= points[other] * coeffs[power]
                coeffs = grown
                scale = scale * (points[column] - points[other])
        for row in range(node_total):
            total = 0.0
            for power in range(len(coeffs)):
                total += coeffs[power] * points[row] ** (power + 1) / (power + 1)
            weights[row][column] = total / scale
    return (weights, [value / node_total for value in points])


def dft_pair(length, direction):
    counter = jnp.arange(length, dtype=jnp.int32)
    phases = (counter[:, None] * counter[None, :] % length).astype(jnp.float32) * (
        2.0 * math.pi / length
    )
    return (jnp.cos(phases), direction * jnp.sin(phases))


def twist_pair(low_factor, high_factor, direction):
    full_length = low_factor * high_factor
    low_counter = jnp.arange(low_factor, dtype=jnp.int32)
    high_counter = jnp.arange(high_factor, dtype=jnp.int32)
    phases = (low_counter[:, None] * high_counter[None, :] % full_length).astype(jnp.float32) * (
        2.0 * math.pi / full_length
    )
    return (jnp.cos(phases), direction * jnp.sin(phases))


def spanwise_transform(real_part, imaginary_part, direction):
    highest = lax.Precision.HIGHEST
    full_length = real_part.shape[-1]
    low_factor = 1
    for candidate in range(1, math.isqrt(full_length) + 1):
        if full_length % candidate == 0:
            low_factor = candidate
    high_factor = full_length // low_factor
    leading = real_part.shape[:-1]
    real_grid = real_part.reshape(leading + (high_factor, low_factor))
    imaginary_grid = imaginary_part.reshape(leading + (high_factor, low_factor))
    cos_high, sin_high = dft_pair(high_factor, direction)
    first_real = jnp.einsum("...rp,rk->...pk", real_grid, cos_high, precision=highest) - jnp.einsum(
        "...rp,rk->...pk", imaginary_grid, sin_high, precision=highest
    )
    first_imaginary = jnp.einsum(
        "...rp,rk->...pk", real_grid, sin_high, precision=highest
    ) + jnp.einsum("...rp,rk->...pk", imaginary_grid, cos_high, precision=highest)
    twist_cos, twist_sin = twist_pair(low_factor, high_factor, direction)
    turned_real = first_real * twist_cos - first_imaginary * twist_sin
    turned_imaginary = first_real * twist_sin + first_imaginary * twist_cos
    cos_low, sin_low = dft_pair(low_factor, direction)
    final_real = jnp.einsum(
        "qp,...pk->...qk", cos_low, turned_real, precision=highest
    ) - jnp.einsum("qp,...pk->...qk", sin_low, turned_imaginary, precision=highest)
    final_imaginary = jnp.einsum(
        "qp,...pk->...qk", sin_low, turned_real, precision=highest
    ) + jnp.einsum("qp,...pk->...qk", cos_low, turned_imaginary, precision=highest)
    normalizer = 1.0 / math.sqrt(full_length)
    return (
        final_real.reshape(leading + (full_length,)) * normalizer,
        final_imaginary.reshape(leading + (full_length,)) * normalizer,
    )


def eigen_apply(matrix, fields):
    return jnp.einsum("yx,mcxq->mcyq", matrix, fields, precision=lax.Precision.HIGHEST)


def plain_local(iterate, start_field, spanwise_velocity, eigen_basis, inverse_basis, decay_rates):
    node_total = lax.axis_size("node") * iterate.shape[0]
    quadrature_table, shift_table = collocation(node_total)
    quadrature = jnp.asarray(quadrature_table, jnp.float32)
    node_index = lax.axis_index("node")
    node_shift = lax.dynamic_index_in_dim(
        jnp.asarray(shift_table, jnp.float32), node_index, 0, keepdims=False
    )
    local_modes = iterate.shape[3]
    full_modes = spanwise_velocity.shape[2]
    wavenumber = lax.axis_index("span") * local_modes + jnp.arange(local_modes, dtype=jnp.int32)
    signed = jnp.where(wavenumber < full_modes // 2, wavenumber, wavenumber - full_modes).astype(jnp.float32) / (
        full_modes // 2
    )
    damping = decay_rates[:, None] + signed[None, :] ** 2
    gradient = jnp.stack([-signed * iterate[:, 1], signed * iterate[:, 0]], axis=1).astype(
        jnp.bfloat16
    )
    span_lines = lax.all_to_all(gradient, "span", split_axis=2, concat_axis=3, tiled=True)
    physical_real, physical_imaginary = spanwise_transform(
        span_lines[:, 0].astype(jnp.float32), span_lines[:, 1].astype(jnp.float32), 1.0
    )
    spectral_real, spectral_imaginary = spanwise_transform(
        -spanwise_velocity * physical_real, -spanwise_velocity * physical_imaginary, -1.0
    )
    advect = jnp.stack([spectral_real, spectral_imaginary], axis=1).astype(jnp.bfloat16)
    wall_terms = lax.all_to_all(advect, "span", split_axis=3, concat_axis=2, tiled=True)
    projected = eigen_apply(inverse_basis, jnp.concatenate([start_field[None], iterate], axis=0))
    section_term = -damping * projected[1:] + eigen_apply(
        inverse_basis, wall_terms.astype(jnp.float32)
    )
    node_major = lax.all_to_all(section_term, "node", split_axis=3, concat_axis=0, tiled=True)
    blended = jnp.einsum("mj,jcyq->mcyq", quadrature, node_major, precision=lax.Precision.HIGHEST)
    summed = lax.all_to_all(blended, "node", split_axis=0, concat_axis=3, tiled=True)[0]
    shifted = node_shift * damping
    new_coeff = (projected[0] + summed + shifted * projected[1]) / (1.0 + shifted)
    return eigen_apply(eigen_basis, new_coeff[None])


LANES = 128
ROWS = 8
CODE_SCALE = 2.0**-6
CHUNKS = ((0, 1, 2), (3, 4, 5), (6, 7, 8))


def split_pair(value):
    high = lax.reduce_precision(value, 8, 7)
    return high.astype(jnp.bfloat16), (value - high).astype(jnp.bfloat16)


def kernel_split(value):
    high = value.astype(jnp.bfloat16)
    return high, (value - high.astype(jnp.float32)).astype(jnp.bfloat16)


def numpy_split(value):
    high = value.astype(jnp.bfloat16)
    low = (value - high.astype(np.float64)).astype(jnp.bfloat16)
    return high, low


def lane_transform(direction):
    index = np.arange(LANES)
    phase = 2.0 * np.pi * (np.outer(index, index) % LANES) / LANES
    cosine, sine = np.cos(phase), direction * np.sin(phase)
    matrix = np.block([[cosine, sine], [-sine, cosine]])
    high, low = numpy_split(matrix)
    return np.concatenate([high, high, low], axis=0)


def twiddle_table(outer, direction, scale):
    full = outer * LANES
    phase = 2.0 * np.pi * (np.outer(np.arange(outer), np.arange(LANES)) % full) / full
    return (
        (scale * np.cos(phase)).astype(np.float32).reshape(outer, 1, LANES),
        (scale * direction * np.sin(phase)).astype(np.float32).reshape(outer, 1, LANES),
    )


def times_i(value, sign):
    return (-value[1], value[0]) if sign > 0 else (value[1], -value[0])


def plus(left, right):
    return (left[0] + right[0], left[1] + right[1])


def minus(left, right):
    return (left[0] - right[0], left[1] - right[1])


def turn(value, angle):
    cosine, sine = np.float32(math.cos(angle)), np.float32(math.sin(angle))
    return (value[0] * cosine - value[1] * sine, value[0] * sine + value[1] * cosine)


def four_points(values, sign):
    even_sum, even_gap = plus(values[0], values[2]), minus(values[0], values[2])
    odd_sum, odd_gap = plus(values[1], values[3]), times_i(minus(values[1], values[3]), sign)
    return [
        plus(even_sum, odd_sum),
        plus(even_gap, odd_gap),
        minus(even_sum, odd_sum),
        minus(even_gap, odd_gap),
    ]


def three_points(values, sign):
    total, gap = plus(values[1], values[2]), minus(values[1], values[2])
    half = np.float32(0.5)
    root = np.float32(math.sqrt(3.0) / 2.0)
    middle = (values[0][0] - half * total[0], values[0][1] - half * total[1])
    side = times_i((root * gap[0], root * gap[1]), sign)
    return [plus(values[0], total), plus(middle, side), minus(middle, side)]


def nine_points(values, sign):
    inner = [three_points([values[3 * b1 + b0] for b1 in range(3)], sign) for b0 in range(3)]
    outs = [None] * 9
    for k0 in range(3):
        turned = [
            inner[b0][k0]
            if b0 * k0 == 0
            else turn(inner[b0][k0], sign * 2.0 * math.pi * b0 * k0 / 9.0)
            for b0 in range(3)
        ]
        for k1, value in enumerate(three_points(turned, sign)):
            outs[k0 + 3 * k1] = value
    return outs


def gradient_kernel(idx_ref, field_ref, signed_ref, *out_refs):
    me = idx_ref[0]
    parity = lax.rem(me, 2)
    modes = field_ref.shape[-1]
    tail = modes % LANES
    full = modes // LANES
    signed = signed_ref[...]

    def emit(shift):
        body = 0 if shift == 0 else tail
        rest = full * LANES if shift == 0 else 0
        for step, out_ref in enumerate(out_refs):
            for other in range(2):
                target = lax.bitwise_xor(me, 2 * step + other)
                real = -signed * field_ref[1, target, 0]
                imaginary = signed * field_ref[0, target, 0]
                for part, value in enumerate((real, imaginary)):
                    shifted = value[:, body : body + full * LANES]
                    for tile in range(full):
                        out_ref[other, part * full + tile] = shifted[
                            :, tile * LANES : (tile + 1) * LANES
                        ].astype(jnp.bfloat16)
                joined = jnp.concatenate(
                    [real[:, rest : rest + tail], imaginary[:, rest : rest + tail]], axis=1
                )
                out_ref[other, 2 * full] = joined.astype(jnp.bfloat16)

    @pl.when(parity == 0)
    def _():
        emit(0)

    @pl.when(parity == 1)
    def _():
        emit(1)


def gradient_blocks(index, field, signed, span_total, unit):
    parts, points, modes = field.shape
    lines = points // span_total
    groups = lines // unit
    tiles = parts * modes // LANES
    view = field.reshape(parts, span_total, groups, unit, modes)
    steps = span_total // 2
    return pl.pallas_call(
        gradient_kernel,
        grid_spec=pltpu.PrefetchScalarGridSpec(
            num_scalar_prefetch=1,
            grid=(groups,),
            in_specs=[
                pl.BlockSpec((parts, span_total, 1, unit, modes), lambda g, i: (0, 0, g, 0, 0)),
                pl.BlockSpec((1, modes), lambda g, i: (0, 0)),
            ],
            out_specs=[pl.BlockSpec((2, tiles, unit, LANES), lambda g, i: (0, 0, g, 0))] * steps,
        ),
        out_shape=[jax.ShapeDtypeStruct((2, tiles, lines, LANES), jnp.bfloat16)] * steps,
        name="gradient",
    )(index, view, signed)


def transform_kernel(idx_ref, *refs):
    steps = 4
    in_refs = refs[:steps]
    got_ref, velocity_ref, back_ref, ahead_ref = refs[steps : steps + 4]
    back_cos, back_sin, ahead_cos, ahead_sin = refs[steps + 4 : steps + 8]
    out_refs = refs[steps + 8 : -2]
    grid_ref, work_ref = refs[-2:]
    me = idx_ref[0]
    chip, core = lax.div(me, 2), lax.rem(me, 2)
    lines = velocity_ref.shape[1]
    outer = velocity_ref.shape[0]
    full = (outer // steps - 1) // 2
    half = LANES // 2
    for step in range(steps):
        other = lax.bitwise_xor(chip, step)
        grid_ref[other, core] = in_refs[step][0].astype(jnp.float32)
        grid_ref[other, 1 - core] = got_ref[step].astype(jnp.float32)
    low_lane = lax.broadcasted_iota(jnp.int32, (ROWS, LANES), 1) < half
    per = outer // steps

    def forward(group, carry):
        rows = pl.ds(pl.multiple_of(group * ROWS, ROWS), ROWS)

        def load(position):
            pair, tile = position // per, position % per
            if tile < full:
                return grid_ref[pair, 0, tile, rows], grid_ref[pair, 0, full + tile, rows]
            if tile > full:
                tile = tile - full - 1
                return grid_ref[pair, 1, tile, rows], grid_ref[pair, 1, full + tile, rows]
            even, odd = grid_ref[pair, 0, 2 * full, rows], grid_ref[pair, 1, 2 * full, rows]
            return (
                jnp.where(low_lane, even, pltpu.roll(odd, half, 1)),
                jnp.where(low_lane, pltpu.roll(even, half, 1), odd),
            )

        columns = [
            four_points([load((9 * a + 4 * b) % outer) for a in range(4)], 1) for b in range(9)
        ]
        for ka in range(4):
            ninth = nine_points([columns[b][ka] for b in range(9)], 1)
            for kb in range(9):
                position = (9 * ka + 28 * kb) % outer
                real, imaginary = ninth[kb]
                cosine, sine = back_cos[position], back_sin[position]
                into = pl.ds(pl.multiple_of(position * lines + group * ROWS, ROWS), ROWS)
                work_ref[into, :LANES] = real * cosine - imaginary * sine
                work_ref[into, LANES:] = real * sine + imaginary * cosine
        return carry

    lax.fori_loop(0, lines // ROWS, forward, 0)

    block = 4
    size = block * lines

    def spread(value):
        high, low = kernel_split(value)
        return jnp.concatenate([high, low, high], axis=1)

    def middle(step, carry):
        rows = pl.ds(pl.multiple_of(step * size, ROWS), size)
        physical = jnp.dot(
            spread(work_ref[rows, :]), back_ref[...], preferred_element_type=jnp.float32
        )
        speed = velocity_ref[pl.ds(step * block, block)].reshape(size, LANES)
        moved = physical * jnp.concatenate([speed, speed], axis=1)
        work_ref[rows, :] = jnp.dot(
            spread(moved), ahead_ref[...], preferred_element_type=jnp.float32
        )
        return carry

    lax.fori_loop(0, outer // block, middle, 0)

    def backward(group, carry):
        rows = pl.ds(pl.multiple_of(group * ROWS, ROWS), ROWS)
        table = [[None] * 9 for _ in range(4)]
        for ka in range(4):
            values = []
            for kb in range(9):
                position = (9 * ka + 28 * kb) % outer
                into = pl.ds(pl.multiple_of(position * lines + group * ROWS, ROWS), ROWS)
                real, imaginary = work_ref[into, :LANES], work_ref[into, LANES:]
                cosine, sine = ahead_cos[position], ahead_sin[position]
                values.append((real * cosine - imaginary * sine, real * sine + imaginary * cosine))
            table[ka] = nine_points(values, -1)
        for b in range(9):
            for a, (real, imaginary) in enumerate(
                four_points([table[ka][b] for ka in range(4)], -1)
            ):
                position = (9 * a + 4 * b) % outer
                pair, tile = position // per, position % per
                if tile < full:
                    grid_ref[pair, 0, tile, rows] = real
                    grid_ref[pair, 0, full + tile, rows] = imaginary
                elif tile > full:
                    tile = tile - full - 1
                    grid_ref[pair, 1, tile, rows] = real
                    grid_ref[pair, 1, full + tile, rows] = imaginary
                else:
                    grid_ref[pair, 0, 2 * full, rows] = jnp.where(
                        low_lane, real, pltpu.roll(imaginary, half, 1)
                    )
                    grid_ref[pair, 1, 2 * full, rows] = jnp.where(
                        low_lane, pltpu.roll(real, half, 1), imaginary
                    )
        return carry

    lax.fori_loop(0, lines // ROWS, backward, 0)

    for step in range(steps):
        other = lax.bitwise_xor(chip, step)
        for place, tiles in enumerate(CHUNKS):
            out_ref = out_refs[place * steps + step]
            for spot, tile in enumerate(tiles):
                out_ref[0, spot] = grid_ref[other, core, tile].astype(jnp.bfloat16)
                out_ref[1, spot] = grid_ref[other, 1 - core, tile].astype(jnp.bfloat16)


def whole(shape):
    return pl.BlockSpec(shape, lambda *_: (0,) * len(shape))


def transform_blocks(index, arrivals, got, velocity):
    outer, lines, _ = velocity.shape
    tiles = arrivals[0].shape[1]
    scale = 1.0 / (outer * LANES)
    tables = (
        lane_transform(1.0),
        lane_transform(-1.0),
        *twiddle_table(outer, 1.0, 1.0),
        *twiddle_table(outer, -1.0, -scale),
    )
    operands = [*arrivals, got, velocity, *(jnp.asarray(t) for t in tables)]
    specs = []
    for value in operands:
        specs.append(whole(value.shape))
    shapes = [
        jax.ShapeDtypeStruct((2, len(t), lines, LANES), jnp.bfloat16)
        for t in CHUNKS
        for _ in range(len(arrivals))
    ]
    return pl.pallas_call(
        transform_kernel,
        grid_spec=pltpu.PrefetchScalarGridSpec(
            num_scalar_prefetch=1,
            grid=(1,),
            in_specs=specs,
            out_specs=[whole(s.shape) for s in shapes],
            scratch_shapes=[
                pltpu.VMEM((len(arrivals), 2, tiles, lines, LANES), jnp.float32),
                pltpu.VMEM((outer * lines, 2 * LANES), jnp.float32),
            ],
        ),
        out_shape=shapes,
        name="transform",
    )(index, *operands)


def pack_into(scratch, source, parity):
    modes = source.shape[-1]
    tail = modes % LANES
    full = modes // LANES

    def emit(body, rest):
        for part in range(2):
            scratch[:, part * full * LANES : (part + 1) * full * LANES] = source[
                part, :, body : body + full * LANES
            ]
        scratch[:, 2 * full * LANES :] = jnp.concatenate(
            [source[0, :, rest : rest + tail], source[1, :, rest : rest + tail]], axis=1
        )

    @pl.when(parity == 0)
    def _():
        emit(0, full * LANES)

    @pl.when(parity == 1)
    def _():
        emit(tail, 0)


def project_kernel(idx_ref, field_ref, matrix_ref, out_ref, pack_ref):
    parity = lax.rem(idx_ref[0], 2)
    pack_into(pack_ref, field_ref, parity)
    high, low = kernel_split(pack_ref[...])
    out_ref[...] = jnp.dot(
        matrix_ref[...],
        jnp.concatenate([high, low, high], axis=0),
        preferred_element_type=jnp.float32,
    )


def project_field(index, field, matrix):
    parts, points, modes = field.shape
    shape = jax.ShapeDtypeStruct((points, parts * modes), jnp.float32)
    return pl.pallas_call(
        project_kernel,
        grid_spec=pltpu.PrefetchScalarGridSpec(
            num_scalar_prefetch=1,
            grid=(1,),
            in_specs=[whole(field.shape), whole(matrix.shape)],
            out_specs=whole(shape.shape),
            scratch_shapes=[pltpu.VMEM(shape.shape, jnp.float32)],
        ),
        out_shape=shape,
        name="project",
    )(index, field, matrix)


def section_kernel(idx_ref, *refs):
    steps = 4
    in_refs = refs[:steps]
    got_ref, matrix_ref, own_ref, decay_ref, square_ref, out_ref, pack_ref = refs[steps:]
    me = idx_ref[0]
    lines = got_ref.shape[2]
    for step in range(steps):
        for other in range(2):
            source = lax.bitwise_xor(me, 2 * step + other)
            block = in_refs[step][0] if other == 0 else got_ref[step]
            rows = pl.ds(pl.multiple_of(source * lines, ROWS), lines)
            for spot in range(block.shape[0]):
                pack_ref[rows, spot * LANES : (spot + 1) * LANES] = block[spot].astype(jnp.float32)
    terms = pack_ref[...].astype(jnp.bfloat16)
    product = jnp.dot(
        matrix_ref[...], jnp.concatenate([terms, terms], axis=0), preferred_element_type=jnp.float32
    )
    damping = decay_ref[...] + square_ref[...]
    out_ref[...] = product - damping * own_ref[...]


def section_chunk(index, arrivals, got, matrix, own, decay, square, tiles):
    points = matrix.shape[0]
    width = len(tiles) * LANES
    place = tiles[0] // len(tiles)
    shape = jax.ShapeDtypeStruct((points, width), jnp.float32)
    operands = [*arrivals, got, matrix, own, decay, square]
    specs = [whole(v.shape) for v in operands[:-3]]
    specs.append(pl.BlockSpec((points, width), lambda *_: (0, place)))
    specs.append(whole(decay.shape))
    specs.append(pl.BlockSpec((1, width), lambda *_: (0, place)))
    return pl.pallas_call(
        section_kernel,
        grid_spec=pltpu.PrefetchScalarGridSpec(
            num_scalar_prefetch=1,
            grid=(1,),
            in_specs=specs,
            out_specs=whole(shape.shape),
            scratch_shapes=[pltpu.VMEM(shape.shape, jnp.float32)],
        ),
        out_shape=shape,
        name="section",
    )(index, *operands)


def update_kernel(idx_ref, shift_ref, *refs):
    count = len(CHUNKS)
    summed_refs = refs[:count]
    own_ref, start_ref, decay_ref, square_ref, matrix_ref, out_ref = refs[count : count + 6]
    pack_ref = refs[-1]
    parity = lax.rem(idx_ref[0], 2)
    for place, tiles in enumerate(CHUNKS):
        columns = slice(tiles[0] * LANES, (tiles[-1] + 1) * LANES)
        shifted = shift_ref[0] * (decay_ref[...] + square_ref[:, columns])
        fresh = (start_ref[:, columns] + summed_refs[place][...] + shifted * own_ref[:, columns]) / (
            1.0 + shifted
        )
        high, low = kernel_split(fresh)
        pack_ref[:, columns] = jnp.dot(
            matrix_ref[...],
            jnp.concatenate([high, low, high], axis=0),
            preferred_element_type=jnp.float32,
        )
    modes = out_ref.shape[-1]
    tail = modes % LANES
    full = modes // LANES
    edge = 2 * full * LANES

    def emit(body, rest):
        for part in range(2):
            out_ref[part, :, body : body + full * LANES] = pack_ref[
                :, part * full * LANES : (part + 1) * full * LANES
            ]
            out_ref[part, :, rest : rest + tail] = pack_ref[
                :, edge + part * tail : edge + (part + 1) * tail
            ]

    @pl.when(parity == 0)
    def _():
        emit(0, full * LANES)

    @pl.when(parity == 1)
    def _():
        emit(tail, 0)


def update_field(index, shift, summed, own, start, decay, square, matrix, modes):
    points = matrix.shape[0]
    shape = jax.ShapeDtypeStruct((2, points, modes), jnp.float32)
    operands = [*summed, own, start, decay, square, matrix]
    return pl.pallas_call(
        update_kernel,
        grid_spec=pltpu.PrefetchScalarGridSpec(
            num_scalar_prefetch=1,
            grid=(1,),
            in_specs=[pl.BlockSpec(memory_space=pltpu.SMEM)] + [whole(v.shape) for v in operands],
            out_specs=whole(shape.shape),
            scratch_shapes=[pltpu.VMEM(own.shape, jnp.float32)],
        ),
        out_shape=shape,
        name="update",
    )(index, shift, *operands)


def flip(value, axis, mask):
    total = lax.axis_size(axis)
    return lax.ppermute(value, axis, [(k, k ^ mask) for k in range(total)])


def span_exchange(blocks):
    arrivals = [blocks[0]] + [flip(blocks[s], "span", 2 * s) for s in (1, 2, 3)]
    got = flip(jnp.stack([block[1] for block in arrivals]), "span", 1)
    return arrivals, got


def fast_local(iterate, start_field, spanwise_velocity, eigen_basis, inverse_basis, decay_rates):
    node_total = lax.axis_size("node")
    span_total = lax.axis_size("span")
    modes = iterate.shape[3]
    full_modes = spanwise_velocity.shape[2]
    lines = spanwise_velocity.shape[1]
    outer = full_modes // LANES
    quadrature_table, shift_table = collocation(node_total)
    node = lax.axis_index("node")
    span = lax.axis_index("span")
    index = span.astype(jnp.int32).reshape(1)
    wavenumber = span * modes + jnp.arange(modes, dtype=jnp.int32)
    signed = jnp.where(
        wavenumber < full_modes // 2, wavenumber, wavenumber - full_modes
    ).astype(jnp.float32) / (full_modes // 2)
    full = modes // LANES
    tail = modes % LANES
    odd = span % 2 == 1
    square = signed**2
    body = jnp.where(odd, square[tail:], square[: full * LANES])
    rest = jnp.where(odd, square[:tail], square[full * LANES :])
    packed_square = jnp.concatenate([body, body, rest, rest])[None]
    decay = decay_rates[:, None]

    blocks = gradient_blocks(index, iterate[0], signed[None], span_total, 24)
    velocity = jnp.transpose(
        spanwise_velocity[0].reshape(lines, LANES, outer), (2, 0, 1)
    )
    inverse_high, inverse_low = split_pair(inverse_basis)
    inverse_three = jnp.concatenate([inverse_high, inverse_high, inverse_low], axis=1)
    inverse_two = jnp.concatenate([inverse_high, inverse_low], axis=1)
    eigen_high, eigen_low = split_pair(eigen_basis)
    eigen_three = jnp.concatenate([eigen_high, eigen_high, eigen_low], axis=1)

    arrivals, got = span_exchange(blocks)
    own = project_field(index, iterate[0], inverse_three)
    start = project_field(index, start_field, inverse_three)
    advect = transform_blocks(index, arrivals, got, velocity)

    weights = jnp.asarray(quadrature_table, jnp.float32)

    def weight(row_mask, column_mask):
        return weights[node ^ row_mask, node ^ column_mask]

    def code(value):
        return (value * CODE_SCALE).astype(jnp.float16)

    def decode(value):
        return value.astype(jnp.float32) * (1.0 / CODE_SCALE)

    summed = []
    steps = span_total // 2
    for place, tiles in enumerate(CHUNKS):
        sent = advect[place * steps : (place + 1) * steps]
        came, partner = span_exchange(sent)
        section = section_chunk(
            index, came, partner, inverse_two, own, decay, packed_square, tiles
        )
        middle = section.shape[0] // 2
        halves = []
        for part, (first, second) in zip((section[:middle], section[middle:]), ((1, 2), (2, 1))):
            near = decode(flip(code(part), "node", first))
            share = weight(second, 0) * part + weight(second, first) * near
            far = decode(flip(code(share), "node", second))
            halves.append(weight(0, 0) * part + weight(0, first) * near + far)
        summed.append(jnp.concatenate(halves, axis=0))
    shift = jnp.asarray(shift_table, jnp.float32)[node].reshape(1)
    updated = update_field(
        index, shift, summed, own, start, decay, packed_square, eigen_three, modes
    )
    return updated[None]


def fits(mesh, shape):
    nodes, span = mesh.shape["node"], mesh.shape["span"]
    node_count, points, full_modes = shape
    if nodes != 4 or span != 8 or node_count != nodes or full_modes % (LANES * span) != LANES // 2 * span:
        return False
    lines = points // span
    return full_modes == 36 * LANES and lines % 24 == 0 and points % span == 0


def solution(mesh):
    placed = (
        P("node", None, None, "span"),
        P(None, None, "span"),
        P("node", "span", None),
        P(),
        P(),
        P(),
    )

    def build(local):
        return jax.shard_map(
            local, mesh=mesh, in_specs=placed, out_specs=P("node", None, None, "span"), check_vma=False
        )

    def run(iterate, start_field, spanwise_velocity, eigen_basis, inverse_basis, decay_rates):
        local = fast_local if fits(mesh, spanwise_velocity.shape) else plain_local
        return build(local)(
            iterate, start_field, spanwise_velocity, eigen_basis, inverse_basis, decay_rates
        )

    return run
```

```python
import functools
import math

import jax
import jax.numpy as jnp
import numpy as np
from jax import lax
from jax.experimental import pallas as pl
from jax.experimental.pallas import tpu as pltpu
from jax.sharding import PartitionSpec as P


def collocation(node_total):
    points = [
        0.5 - 0.5 * math.cos((2.0 * m + 1.0) * math.pi / (2.0 * node_total))
        for m in range(node_total)
    ]
    weights = [[0.0] * node_total for _ in range(node_total)]
    for column in range(node_total):
        coeffs = [1.0]
        scale = 1.0
        for other in range(node_total):
            if other != column:
                grown = [0.0] * (len(coeffs) + 1)
                for power in range(len(coeffs)):
                    grown[power + 1] += coeffs[power]
                    grown[power] -= points[other] * coeffs[power]
                coeffs = grown
                scale = scale * (points[column] - points[other])
        for row in range(node_total):
            total = 0.0
            for power in range(len(coeffs)):
                total += coeffs[power] * points[row] ** (power + 1) / (power + 1)
            weights[row][column] = total / scale
    return (weights, [value / node_total for value in points])


def dft_pair(length, direction):
    counter = jnp.arange(length, dtype=jnp.int32)
    phases = (counter[:, None] * counter[None, :] % length).astype(jnp.float32) * (
        2.0 * math.pi / length
    )
    return (jnp.cos(phases), direction * jnp.sin(phases))


def twist_pair(low_factor, high_factor, direction):
    full_length = low_factor * high_factor
    low_counter = jnp.arange(low_factor, dtype=jnp.int32)
    high_counter = jnp.arange(high_factor, dtype=jnp.int32)
    phases = (low_counter[:, None] * high_counter[None, :] % full_length).astype(jnp.float32) * (
        2.0 * math.pi / full_length
    )
    return (jnp.cos(phases), direction * jnp.sin(phases))


def spanwise_transform(real_part, imaginary_part, direction):
    highest = lax.Precision.HIGHEST
    full_length = real_part.shape[-1]
    low_factor = 1
    for candidate in range(1, math.isqrt(full_length) + 1):
        if full_length % candidate == 0:
            low_factor = candidate
    high_factor = full_length // low_factor
    leading = real_part.shape[:-1]
    real_grid = real_part.reshape(leading + (high_factor, low_factor))
    imaginary_grid = imaginary_part.reshape(leading + (high_factor, low_factor))
    cos_high, sin_high = dft_pair(high_factor, direction)
    first_real = jnp.einsum("...rp,rk->...pk", real_grid, cos_high, precision=highest) - jnp.einsum(
        "...rp,rk->...pk", imaginary_grid, sin_high, precision=highest
    )
    first_imaginary = jnp.einsum(
        "...rp,rk->...pk", real_grid, sin_high, precision=highest
    ) + jnp.einsum("...rp,rk->...pk", imaginary_grid, cos_high, precision=highest)
    twist_cos, twist_sin = twist_pair(low_factor, high_factor, direction)
    turned_real = first_real * twist_cos - first_imaginary * twist_sin
    turned_imaginary = first_real * twist_sin + first_imaginary * twist_cos
    cos_low, sin_low = dft_pair(low_factor, direction)
    final_real = jnp.einsum(
        "qp,...pk->...qk", cos_low, turned_real, precision=highest
    ) - jnp.einsum("qp,...pk->...qk", sin_low, turned_imaginary, precision=highest)
    final_imaginary = jnp.einsum(
        "qp,...pk->...qk", sin_low, turned_real, precision=highest
    ) + jnp.einsum("qp,...pk->...qk", cos_low, turned_imaginary, precision=highest)
    normalizer = 1.0 / math.sqrt(full_length)
    return (
        final_real.reshape(leading + (full_length,)) * normalizer,
        final_imaginary.reshape(leading + (full_length,)) * normalizer,
    )


def eigen_apply(matrix, fields):
    return jnp.einsum("yx,mcxq->mcyq", matrix, fields, precision=lax.Precision.HIGHEST)


def plain_local(iterate, start_field, spanwise_velocity, eigen_basis, inverse_basis, decay_rates):
    node_total = lax.axis_size("node") * iterate.shape[0]
    quadrature_table, shift_table = collocation(node_total)
    quadrature = jnp.asarray(quadrature_table, jnp.float32)
    node_index = lax.axis_index("node")
    node_shift = lax.dynamic_index_in_dim(
        jnp.asarray(shift_table, jnp.float32), node_index, 0, keepdims=False
    )
    local_modes = iterate.shape[3]
    full_modes = spanwise_velocity.shape[2]
    wavenumber = lax.axis_index("span") * local_modes + jnp.arange(local_modes, dtype=jnp.int32)
    signed = jnp.where(wavenumber < full_modes // 2, wavenumber, wavenumber - full_modes).astype(jnp.float32) / (
        full_modes // 2
    )
    damping = decay_rates[:, None] + signed[None, :] ** 2
    gradient = jnp.stack([-signed * iterate[:, 1], signed * iterate[:, 0]], axis=1).astype(
        jnp.bfloat16
    )
    span_lines = lax.all_to_all(gradient, "span", split_axis=2, concat_axis=3, tiled=True)
    physical_real, physical_imaginary = spanwise_transform(
        span_lines[:, 0].astype(jnp.float32), span_lines[:, 1].astype(jnp.float32), 1.0
    )
    spectral_real, spectral_imaginary = spanwise_transform(
        -spanwise_velocity * physical_real, -spanwise_velocity * physical_imaginary, -1.0
    )
    advect = jnp.stack([spectral_real, spectral_imaginary], axis=1).astype(jnp.bfloat16)
    wall_terms = lax.all_to_all(advect, "span", split_axis=3, concat_axis=2, tiled=True)
    projected = eigen_apply(inverse_basis, jnp.concatenate([start_field[None], iterate], axis=0))
    section_term = -damping * projected[1:] + eigen_apply(
        inverse_basis, wall_terms.astype(jnp.float32)
    )
    node_major = lax.all_to_all(section_term, "node", split_axis=3, concat_axis=0, tiled=True)
    blended = jnp.einsum("mj,jcyq->mcyq", quadrature, node_major, precision=lax.Precision.HIGHEST)
    summed = lax.all_to_all(blended, "node", split_axis=0, concat_axis=3, tiled=True)[0]
    shifted = node_shift * damping
    new_coeff = (projected[0] + summed + shifted * projected[1]) / (1.0 + shifted)
    return eigen_apply(eigen_basis, new_coeff[None])


LANES = 128
ROWS = 8
CODE_SCALE = 2.0**-6
CHUNKS = ((0, 1, 2), (3, 4, 5), (6, 7, 8))


def split_pair(value):
    high = lax.reduce_precision(value, 8, 7)
    return high.astype(jnp.bfloat16), (value - high).astype(jnp.bfloat16)


def kernel_split(value):
    high = value.astype(jnp.bfloat16)
    return high, (value - high.astype(jnp.float32)).astype(jnp.bfloat16)


def numpy_split(value):
    high = value.astype(jnp.bfloat16)
    low = (value - high.astype(np.float64)).astype(jnp.bfloat16)
    return high, low


def lane_transform(direction):
    index = np.arange(LANES)
    phase = 2.0 * np.pi * (np.outer(index, index) % LANES) / LANES
    cosine, sine = np.cos(phase), direction * np.sin(phase)
    matrix = np.block([[cosine, sine], [-sine, cosine]])
    high, low = numpy_split(matrix)
    return np.concatenate([high, high, low], axis=0)


def twiddle_table(outer, direction, scale):
    full = outer * LANES
    phase = 2.0 * np.pi * (np.outer(np.arange(outer), np.arange(LANES)) % full) / full
    return (
        (scale * np.cos(phase)).astype(np.float32).reshape(outer, 1, LANES),
        (scale * direction * np.sin(phase)).astype(np.float32).reshape(outer, 1, LANES),
    )


def times_i(value, sign):
    return (-value[1], value[0]) if sign > 0 else (value[1], -value[0])


def plus(left, right):
    return (left[0] + right[0], left[1] + right[1])


def minus(left, right):
    return (left[0] - right[0], left[1] - right[1])


def turn(value, angle):
    cosine, sine = np.float32(math.cos(angle)), np.float32(math.sin(angle))
    return (value[0] * cosine - value[1] * sine, value[0] * sine + value[1] * cosine)


def four_points(values, sign):
    even_sum, even_gap = plus(values[0], values[2]), minus(values[0], values[2])
    odd_sum, odd_gap = plus(values[1], values[3]), times_i(minus(values[1], values[3]), sign)
    return [
        plus(even_sum, odd_sum),
        plus(even_gap, odd_gap),
        minus(even_sum, odd_sum),
        minus(even_gap, odd_gap),
    ]


def three_points(values, sign):
    total, gap = plus(values[1], values[2]), minus(values[1], values[2])
    half = np.float32(0.5)
    root = np.float32(math.sqrt(3.0) / 2.0)
    middle = (values[0][0] - half * total[0], values[0][1] - half * total[1])
    side = times_i((root * gap[0], root * gap[1]), sign)
    return [plus(values[0], total), plus(middle, side), minus(middle, side)]


def nine_points(values, sign):
    inner = [three_points([values[3 * b1 + b0] for b1 in range(3)], sign) for b0 in range(3)]
    outs = [None] * 9
    for k0 in range(3):
        turned = [
            inner[b0][k0]
            if b0 * k0 == 0
            else turn(inner[b0][k0], sign * 2.0 * math.pi * b0 * k0 / 9.0)
            for b0 in range(3)
        ]
        for k1, value in enumerate(three_points(turned, sign)):
            outs[k0 + 3 * k1] = value
    return outs


def gradient_kernel(idx_ref, field_ref, signed_ref, *out_refs):
    me = idx_ref[0]
    parity = lax.rem(me, 2)
    modes = field_ref.shape[-1]
    tail = modes % LANES
    full = modes // LANES
    signed = signed_ref[...]

    def emit(shift):
        body = 0 if shift == 0 else tail
        rest = full * LANES if shift == 0 else 0
        for step, out_ref in enumerate(out_refs):
            for other in range(2):
                target = lax.bitwise_xor(me, 2 * step + other)
                real = -signed * field_ref[1, target, 0]
                imaginary = signed * field_ref[0, target, 0]
                for part, value in enumerate((real, imaginary)):
                    shifted = value[:, body : body + full * LANES]
                    for tile in range(full):
                        out_ref[other, part * full + tile] = shifted[
                            :, tile * LANES : (tile + 1) * LANES
                        ].astype(jnp.bfloat16)
                joined = jnp.concatenate(
                    [real[:, rest : rest + tail], imaginary[:, rest : rest + tail]], axis=1
                )
                out_ref[other, 2 * full] = joined.astype(jnp.bfloat16)

    @pl.when(parity == 0)
    def _():
        emit(0)

    @pl.when(parity == 1)
    def _():
        emit(1)


def gradient_blocks(index, field, signed, span_total, unit):
    parts, points, modes = field.shape
    lines = points // span_total
    groups = lines // unit
    tiles = parts * modes // LANES
    view = field.reshape(parts, span_total, groups, unit, modes)
    steps = span_total // 2
    return pl.pallas_call(
        gradient_kernel,
        grid_spec=pltpu.PrefetchScalarGridSpec(
            num_scalar_prefetch=1,
            grid=(groups,),
            in_specs=[
                pl.BlockSpec((parts, span_total, 1, unit, modes), lambda g, i: (0, 0, g, 0, 0)),
                pl.BlockSpec((1, modes), lambda g, i: (0, 0)),
            ],
            out_specs=[pl.BlockSpec((2, tiles, unit, LANES), lambda g, i: (0, 0, g, 0))] * steps,
        ),
        out_shape=[jax.ShapeDtypeStruct((2, tiles, lines, LANES), jnp.bfloat16)] * steps,
        name="gradient",
    )(index, view, signed)


def transform_kernel(idx_ref, *refs):
    steps = 4
    in_refs = refs[:steps]
    got_ref, velocity_ref, back_ref, ahead_ref = refs[steps : steps + 4]
    back_cos, back_sin, ahead_cos, ahead_sin = refs[steps + 4 : steps + 8]
    out_refs = refs[steps + 9 : -2]
    grid_ref, work_ref = refs[-2:]
    me = idx_ref[0]
    chip, core = lax.div(me, 2), lax.rem(me, 2)
    lines = velocity_ref.shape[1]
    outer = velocity_ref.shape[0]
    full = (outer // steps - 1) // 2
    half = LANES // 2
    for step in range(steps):
        other = lax.bitwise_xor(chip, step)
        grid_ref[other, core] = in_refs[step][0].astype(jnp.float32)
        grid_ref[other, 1 - core] = got_ref[step].astype(jnp.float32)
    low_lane = lax.broadcasted_iota(jnp.int32, (ROWS, LANES), 1) < half
    per = outer // steps

    def forward(group, carry):
        rows = pl.ds(pl.multiple_of(group * ROWS, ROWS), ROWS)

        def load(position):
            pair, tile = position // per, position % per
            if tile < full:
                return grid_ref[pair, 0, tile, rows], grid_ref[pair, 0, full + tile, rows]
            if tile > full:
                tile = tile - full - 1
                return grid_ref[pair, 1, tile, rows], grid_ref[pair, 1, full + tile, rows]
            even, odd = grid_ref[pair, 0, 2 * full, rows], grid_ref[pair, 1, 2 * full, rows]
            return (
                jnp.where(low_lane, even, pltpu.roll(odd, half, 1)),
                jnp.where(low_lane, pltpu.roll(even, half, 1), odd),
            )

        columns = [
            four_points([load((9 * a + 4 * b) % outer) for a in range(4)], 1) for b in range(9)
        ]
        for ka in range(4):
            ninth = nine_points([columns[b][ka] for b in range(9)], 1)
            for kb in range(9):
                position = (9 * ka + 28 * kb) % outer
                real, imaginary = ninth[kb]
                cosine, sine = back_cos[position], back_sin[position]
                into = pl.ds(pl.multiple_of(position * lines + group * ROWS, ROWS), ROWS)
                work_ref[into, :LANES] = real * cosine - imaginary * sine
                work_ref[into, LANES:] = real * sine + imaginary * cosine
        return carry

    lax.fori_loop(0, lines // ROWS, forward, 0)

    block = 4
    size = block * lines

    def spread(value):
        high, low = kernel_split(value)
        return jnp.concatenate([high, low, high], axis=1)

    def middle(step, carry):
        rows = pl.ds(pl.multiple_of(step * size, ROWS), size)
        physical = jnp.dot(
            spread(work_ref[rows, :]), back_ref[...], preferred_element_type=jnp.float32
        )
        speed = velocity_ref[pl.ds(step * block, block)].reshape(size, LANES)
        moved = physical * jnp.concatenate([speed, speed], axis=1)
        work_ref[rows, :] = jnp.dot(
            spread(moved), ahead_ref[...], preferred_element_type=jnp.float32
        )
        return carry

    lax.fori_loop(0, outer // block, middle, 0)

    def backward(group, carry):
        rows = pl.ds(pl.multiple_of(group * ROWS, ROWS), ROWS)
        table = [[None] * 9 for _ in range(4)]
        for ka in range(4):
            values = []
            for kb in range(9):
                position = (9 * ka + 28 * kb) % outer
                into = pl.ds(pl.multiple_of(position * lines + group * ROWS, ROWS), ROWS)
                real, imaginary = work_ref[into, :LANES], work_ref[into, LANES:]
                cosine, sine = ahead_cos[position], ahead_sin[position]
                values.append((real * cosine - imaginary * sine, real * sine + imaginary * cosine))
            table[ka] = nine_points(values, -1)
        for b in range(9):
            for a, (real, imaginary) in enumerate(
                four_points([table[ka][b] for ka in range(4)], -1)
            ):
                position = (9 * a + 4 * b) % outer
                pair, tile = position // per, position % per
                if tile < full:
                    grid_ref[pair, 0, tile, rows] = real
                    grid_ref[pair, 0, full + tile, rows] = imaginary
                elif tile > full:
                    tile = tile - full - 1
                    grid_ref[pair, 1, tile, rows] = real
                    grid_ref[pair, 1, full + tile, rows] = imaginary
                else:
                    grid_ref[pair, 0, 2 * full, rows] = jnp.where(
                        low_lane, real, pltpu.roll(imaginary, half, 1)
                    )
                    grid_ref[pair, 1, 2 * full, rows] = jnp.where(
                        low_lane, pltpu.roll(real, half, 1), imaginary
                    )
        return carry

    lax.fori_loop(0, lines // ROWS, backward, 0)

    for step in range(steps):
        other = lax.bitwise_xor(chip, step)
        for place, tiles in enumerate(CHUNKS):
            out_ref = out_refs[place * steps + step]
            for spot, tile in enumerate(tiles):
                out_ref[0, spot] = grid_ref[other, core, tile].astype(jnp.bfloat16)
                out_ref[1, spot] = grid_ref[other, 1 - core, tile].astype(jnp.bfloat16)


def whole(_=None):
    return pl.BlockSpec(memory_space=pltpu.VMEM)


def unread():
    return pl.BlockSpec(memory_space=pl.ANY)


def transform_blocks(index, arrivals, got, velocity, after):
    outer, lines, _ = velocity.shape
    tiles = arrivals[0].shape[1]
    scale = 1.0 / (outer * LANES)
    tables = (
        lane_transform(1.0),
        lane_transform(-1.0),
        *twiddle_table(outer, 1.0, 1.0),
        *twiddle_table(outer, -1.0, -scale),
    )
    operands = [*arrivals, got, velocity, *(jnp.asarray(t) for t in tables)]
    specs = [whole() for _ in operands] + [unread()]
    operands.append(after)
    shapes = [
        jax.ShapeDtypeStruct((2, len(t), lines, LANES), jnp.bfloat16)
        for t in CHUNKS
        for _ in range(len(arrivals))
    ]
    return pl.pallas_call(
        transform_kernel,
        grid_spec=pltpu.PrefetchScalarGridSpec(
            num_scalar_prefetch=1,
            grid=(1,),
            in_specs=specs,
            out_specs=[whole(s.shape) for s in shapes],
            scratch_shapes=[
                pltpu.VMEM((len(arrivals), 2, tiles, lines, LANES), jnp.float32),
                pltpu.VMEM((outer * lines, 2 * LANES), jnp.float32),
            ],
        ),
        out_shape=shapes,
        name="transform",
    )(index, *operands)


def velocity_kernel(in_ref, out_ref, turned_ref):
    lines, modes = in_ref.shape
    outer = modes // LANES
    for tile in range(outer):
        turned_ref[tile * LANES : (tile + 1) * LANES, :] = in_ref[
            :, tile * LANES : (tile + 1) * LANES
        ].T
    for place in range(outer):
        out_ref[place] = turned_ref[pl.ds(place, LANES, stride=outer), :].T


def turn_velocity(velocity):
    lines, modes = velocity.shape
    return pl.pallas_call(
        velocity_kernel,
        in_specs=[whole()],
        out_specs=whole(),
        scratch_shapes=[pltpu.VMEM((modes, lines), jnp.float32)],
        out_shape=jax.ShapeDtypeStruct((modes // LANES, lines, LANES), jnp.float32),
        name="velocity",
    )(velocity)


def pack_into(scratch, source, parity):
    modes = source.shape[-1]
    tail = modes % LANES
    full = modes // LANES

    def emit(body, rest):
        for part in range(2):
            scratch[:, part * full * LANES : (part + 1) * full * LANES] = source[
                part, :, body : body + full * LANES
            ]
        scratch[:, 2 * full * LANES :] = jnp.concatenate(
            [source[0, :, rest : rest + tail], source[1, :, rest : rest + tail]], axis=1
        )

    @pl.when(parity == 0)
    def _():
        emit(0, full * LANES)

    @pl.when(parity == 1)
    def _():
        emit(tail, 0)


def triple(value):
    high, low = kernel_split(value)
    return jnp.concatenate([high, low, high], axis=0)


def project_kernel(
    idx_ref,
    shift_ref,
    field_ref,
    start_ref,
    inverse_ref,
    eigen_ref,
    decay_ref,
    square_ref,
    damped_ref,
    base_ref,
    inverse_two_ref,
    eigen_three_ref,
    first_ref,
    second_ref,
    matrix_ref,
):
    parity = lax.rem(idx_ref[0], 2)
    points = inverse_ref.shape[0]
    for source, target in ((inverse_ref, matrix_ref), (eigen_ref, eigen_three_ref)):
        high, low = kernel_split(source[...])
        target[:, :points] = high
        target[:, points : 2 * points] = high
        target[:, 2 * points :] = low
        if source is inverse_ref:
            inverse_two_ref[:, :points] = high
            inverse_two_ref[:, points:] = low
    pack_into(first_ref, field_ref, parity)
    pack_into(second_ref, start_ref, parity)
    width = first_ref.shape[1]
    step = 3 * LANES
    for left in range(0, width, step):
        columns = slice(left, left + step)
        damping = decay_ref[...] + square_ref[:, columns]
        matrix = matrix_ref[...]
        own = jnp.dot(matrix, triple(first_ref[:, columns]), preferred_element_type=jnp.float32)
        start = jnp.dot(matrix, triple(second_ref[:, columns]), preferred_element_type=jnp.float32)
        damped = damping * own
        damped_ref[:, columns] = damped
        base_ref[:, columns] = start + shift_ref[0] * damped


def project_fields(index, shift, field, start, inverse, eigen, decay, square):
    parts, points, modes = field.shape
    width = parts * modes
    shapes = [
        jax.ShapeDtypeStruct((points, width), jnp.float32),
        jax.ShapeDtypeStruct((points, width), jnp.float32),
        jax.ShapeDtypeStruct((points, 2 * points), jnp.bfloat16),
        jax.ShapeDtypeStruct((points, 3 * points), jnp.bfloat16),
    ]
    return pl.pallas_call(
        project_kernel,
        in_specs=[pl.BlockSpec(memory_space=pltpu.SMEM)] * 2 + [whole()] * 6,
        out_specs=[whole()] * 4,
        scratch_shapes=[
            pltpu.VMEM((points, width), jnp.float32),
            pltpu.VMEM((points, width), jnp.float32),
            pltpu.VMEM((points, 3 * points), jnp.bfloat16),
        ],
        out_shape=shapes,
        name="project",
    )(index, shift, field, start, inverse, eigen, decay, square)


def section_kernel(tiles, idx_ref, weight_ref, *refs):
    steps = 4
    in_refs = refs[:steps]
    got_ref, matrix_ref, damped_ref, base_ref = refs[steps : steps + 4]
    out_refs = refs[steps + 4 : -1]
    pack_ref = refs[-1]
    me = idx_ref[0]
    lines = got_ref.shape[2]
    for step in range(steps):
        for other in range(2):
            source = lax.bitwise_xor(me, 2 * step + other)
            rows = pl.ds(pl.multiple_of(source * lines, ROWS), lines)
            for spot in range(len(tiles)):
                block = in_refs[step][0, spot] if other == 0 else got_ref[step, spot]
                pack_ref[rows, spot * LANES : (spot + 1) * LANES] = block.astype(jnp.float32)
    terms = pack_ref[...].astype(jnp.bfloat16)
    columns = slice(tiles[0] * LANES, (tiles[-1] + 1) * LANES)
    product = jnp.dot(
        matrix_ref[...], jnp.concatenate([terms, terms], axis=0), preferred_element_type=jnp.float32
    )
    section = product - damped_ref[:, columns]
    mixed = base_ref[:, columns] + weight_ref[0] * section
    middle = section.shape[0] // 2
    out_refs[0][...] = section[:middle]
    out_refs[1][...] = section[middle:]
    out_refs[2][...] = mixed[:middle]
    out_refs[3][...] = mixed[middle:]


def section_chunk(index, weight, arrivals, got, matrix, damped, base, tiles):
    points = matrix.shape[0]
    width = len(tiles) * LANES
    shape = jax.ShapeDtypeStruct((points // 2, width), jnp.float32)
    operands = [*arrivals, got, matrix, damped, base]
    return pl.pallas_call(
        functools.partial(section_kernel, tiles),
        in_specs=[pl.BlockSpec(memory_space=pltpu.SMEM)] * 2 + [whole()] * len(operands),
        out_specs=[whole()] * 4,
        scratch_shapes=[pltpu.VMEM((points, width), jnp.float32)],
        out_shape=[shape] * 4,
        name="section",
    )(index, weight, *operands)


def fresh_terms(low_ref, high_ref, shift, decay_ref, square):
    mixed = jnp.concatenate([low_ref[...], high_ref[...]], axis=0)
    return triple(mixed / (1.0 + shift * (decay_ref[...] + square)))


def update_kernel(tiles, shift_ref, low_ref, high_ref, decay_ref, square_ref, matrix_ref, out_ref):
    columns = slice(tiles[0] * LANES, (tiles[-1] + 1) * LANES)
    fresh = fresh_terms(low_ref, high_ref, shift_ref[0], decay_ref, square_ref[:, columns])
    out_ref[...] = jnp.dot(matrix_ref[...], fresh, preferred_element_type=jnp.float32)


def update_chunk(shift, halves, decay, square, matrix, tiles):
    points = matrix.shape[0]
    return pl.pallas_call(
        functools.partial(update_kernel, tiles),
        in_specs=[pl.BlockSpec(memory_space=pltpu.SMEM)] + [whole()] * 5,
        out_specs=whole(),
        out_shape=jax.ShapeDtypeStruct((points, len(tiles) * LANES), jnp.float32),
        name="update",
    )(shift, *halves, decay, square, matrix)


def last_kernel(
    idx_ref, shift_ref, *refs
):
    count = len(CHUNKS) - 1
    done_refs = refs[:count]
    low_ref, high_ref, decay_ref, square_ref, matrix_ref, out_ref, fresh_ref, pack_ref = refs[count:]
    tiles = CHUNKS[-1]
    columns = slice(tiles[0] * LANES, (tiles[-1] + 1) * LANES)
    step = pl.program_id(0)
    height = out_ref.shape[1]

    @pl.when(step == 0)
    def _():
        fresh_ref[...] = fresh_terms(
            low_ref, high_ref, shift_ref[0], decay_ref, square_ref[:, columns]
        )

    rows = pl.ds(pl.multiple_of(step * height, ROWS), height)
    for place, done_ref in enumerate(done_refs):
        own = CHUNKS[place]
        pack_ref[:, own[0] * LANES : (own[-1] + 1) * LANES] = done_ref[rows, :]
    pack_ref[:, columns] = jnp.dot(
        matrix_ref[rows, :], fresh_ref[...], preferred_element_type=jnp.float32
    )
    modes = out_ref.shape[-1]
    tail = modes % LANES
    full = modes // LANES
    edge = 2 * full * LANES

    def emit(body, rest):
        for part in range(2):
            out_ref[part, :, body : body + full * LANES] = pack_ref[
                :, part * full * LANES : (part + 1) * full * LANES
            ]
            out_ref[part, :, rest : rest + tail] = pack_ref[
                :, edge + part * tail : edge + (part + 1) * tail
            ]

    parity = lax.rem(idx_ref[0], 2)

    @pl.when(parity == 0)
    def _():
        emit(0, full * LANES)

    @pl.when(parity == 1)
    def _():
        emit(tail, 0)


def last_chunk(index, shift, done, halves, decay, square, matrix, modes):
    points = matrix.shape[0]
    width = len(CHUNKS[-1]) * LANES
    blocks = 4
    height = points // blocks
    operands = [*done, *halves, decay, square, matrix]
    return pl.pallas_call(
        last_kernel,
        grid=(blocks,),
        in_specs=[pl.BlockSpec(memory_space=pltpu.SMEM)] * 2 + [whole()] * len(operands),
        out_specs=pl.BlockSpec((2, height, modes), lambda r: (0, r, 0)),
        scratch_shapes=[
            pltpu.VMEM((3 * points, width), jnp.bfloat16),
            pltpu.VMEM((height, square.shape[1]), jnp.float32),
        ],
        out_shape=jax.ShapeDtypeStruct((2, points, modes), jnp.float32),
        name="last",
    )(index, shift, *operands)


def flip(value, axis, mask):
    total = lax.axis_size(axis)
    return lax.ppermute(value, axis, [(k, k ^ mask) for k in range(total)])


def span_exchange(blocks):
    arrivals = [blocks[0]] + [flip(blocks[s], "span", 2 * s) for s in (1, 2, 3)]
    got = flip(jnp.stack([block[1] for block in arrivals]), "span", 1)
    return arrivals, got


def fast_local(iterate, start_field, spanwise_velocity, eigen_basis, inverse_basis, decay_rates):
    node_total = lax.axis_size("node")
    span_total = lax.axis_size("span")
    modes = iterate.shape[3]
    full_modes = spanwise_velocity.shape[2]
    lines = spanwise_velocity.shape[1]
    outer = full_modes // LANES
    quadrature_table, shift_table = collocation(node_total)
    node = lax.axis_index("node")
    span = lax.axis_index("span")
    index = span.astype(jnp.int32).reshape(1)
    wavenumber = span * modes + jnp.arange(modes, dtype=jnp.int32)
    signed = jnp.where(
        wavenumber < full_modes // 2, wavenumber, wavenumber - full_modes
    ).astype(jnp.float32) / (full_modes // 2)
    full = modes // LANES
    tail = modes % LANES
    odd = span % 2 == 1
    square = signed**2
    body = jnp.where(odd, square[tail:], square[: full * LANES])
    rest = jnp.where(odd, square[:tail], square[full * LANES :])
    packed_square = jnp.concatenate([body, body, rest, rest])[None]
    decay = decay_rates[:, None]

    shift = jnp.asarray(shift_table, jnp.float32)[node].reshape(1)
    blocks = gradient_blocks(index, iterate[0], signed[None], span_total, 24)
    velocity = turn_velocity(spanwise_velocity[0])
    damped, base, inverse_two, eigen_three = project_fields(
        index, shift, iterate[0], start_field, inverse_basis, eigen_basis, decay, packed_square
    )
    arrivals, got = span_exchange(blocks)
    advect = transform_blocks(index, arrivals, got, velocity, base)

    weights = jnp.asarray(quadrature_table, jnp.float32)

    def weight(row_mask, column_mask):
        return weights[node ^ row_mask, node ^ column_mask]

    def code(value):
        return (value * CODE_SCALE).astype(jnp.float16)

    def decode(value):
        return value.astype(jnp.float32) * (1.0 / CODE_SCALE)

    own_weight = weight(0, 0).reshape(1)
    steps = span_total // 2
    done = []
    for place, tiles in enumerate(CHUNKS):
        came, partner = span_exchange(advect[place * steps : (place + 1) * steps])
        pieces = section_chunk(
            index, own_weight, came, partner, inverse_two, damped, base, tiles
        )
        halves = []
        for part, mixed, (first, second) in zip(pieces[:2], pieces[2:], ((1, 2), (2, 1))):
            near = decode(flip(code(part), "node", first))
            share = weight(second, 0) * part + weight(second, first) * near
            far = decode(flip(code(share), "node", second))
            halves.append(mixed + weight(0, first) * near + far)
        if place < len(CHUNKS) - 1:
            done.append(update_chunk(shift, halves, decay, packed_square, eigen_three, tiles))
    updated = last_chunk(
        index, shift, done, halves, decay, packed_square, eigen_three, modes
    )
    return updated[None]


def fits(mesh, shape):
    nodes, span = mesh.shape["node"], mesh.shape["span"]
    node_count, points, full_modes = shape
    if nodes != 4 or span != 8 or node_count != nodes or full_modes % (LANES * span) != LANES // 2 * span:
        return False
    lines = points // span
    return full_modes == 36 * LANES and lines % 24 == 0 and points % span == 0


def solution(mesh):
    placed = (
        P("node", None, None, "span"),
        P(None, None, "span"),
        P("node", "span", None),
        P(),
        P(),
        P(),
    )

    def build(local):
        return jax.shard_map(
            local, mesh=mesh, in_specs=placed, out_specs=P("node", None, None, "span"), check_vma=False
        )

    def run(iterate, start_field, spanwise_velocity, eigen_basis, inverse_basis, decay_rates):
        local = fast_local if fits(mesh, spanwise_velocity.shape) else plain_local
        return build(local)(
            iterate, start_field, spanwise_velocity, eigen_basis, inverse_basis, decay_rates
        )

    return run
```
